32 devices in a mesh: aa: 4 (over z), ba: 8 (over y, x, core).
Axes of the slice: x: 2, y: 2, z: 4, core: 2. Of those that a mesh axis runs over, the one named last changes fastest.
Arguments:
- feats: bfloat16 [4, 32, 128, 256], P('aa', 'ba'), may hold values from -6 to 6
- conv_one: bfloat16 [3, 3, 3, 256, 256], replicated, may hold values from -0.078125 to 0.078125
- bias_one: float32 [256], replicated, may hold values from -3 to 3
- conv_two: bfloat16 [3, 3, 3, 256, 256], replicated, may hold values from -0.078125 to 0.078125
- bias_two: float32 [256], replicated, may hold values from -3 to 3
- patch_weight: bfloat16 [2, 2, 256, 128], replicated, may hold values from -0.1875 to 0.1875
- patch_bias: float32 [128], replicated, may hold values from -3 to 3
- embed_weight: bfloat16 [128, 2048], replicated, may hold values from -0.5 to 0.5
- embed_bias: float32 [2048], replicated, may hold values from -6 to 6
- norm_gain: float32 [2048], replicated, may hold values from 0.1 to 1.9
- w_query: bfloat16 [2048, 2048], P(None, 'ba'), may hold values from -2 to 2
- w_key: bfloat16 [2048, 2048], P(None, 'ba'), may hold values from -2 to 2
- w_value: bfloat16 [2048, 2048], P(None, 'ba'), may hold values from -0.125 to 0.125
- w_velocity: bfloat16 [2048, 128], P('ba'), may hold values from -0.5 to 0.5
Outputs:
- velocity: float32 [4096, 128], P(('aa', 'ba'))
The draws below stay inside these ranges and needn't reach their ends.
All inputs are finite; a program needn't handle non-finite values.
Results may differ from the reference program's by a relative error of at most 0.035.
Values may be sent and summed in bfloat16 or wider, within the bound.
A program may use at most 128 MiB of HBM per device.

```python
import math
import jax
import jax.numpy as jnp
from jax import lax

C = 256
LAT = 128
D = 2048
HEADS = 32
HEAD_DIM = 64
FT = 1
SH = 4
W = 128
TOKENS = 4096
FRAMES = 4
ROWS = 32
N_AA = 4
N_BA = 8


def shared_query(key):
    return jax.random.normal(jax.random.fold_in(key, 11), (D, D), jnp.float32) * D ** (-0.5)


def draw_w_query(key, part):
    return jnp.clip(shared_query(key), -2.0, 2.0).astype(jnp.bfloat16)


def draw_w_key(key, part):
    noise = jax.random.normal(jax.random.fold_in(key, 23), (D, D), jnp.float32) * (4.0 * D ** (-0.5))
    return jnp.clip(noise, -2.0, 2.0).astype(jnp.bfloat16)


def levels(own_key, dims, cuts, smallest, high):
    def one(axis_at, blocks):
        draws = jax.random.uniform(jax.random.fold_in(jax.random.fold_in(own_key, 6), axis_at), (blocks,), jnp.float32, smallest / len(cuts), high / len(cuts))
        return jnp.repeat(jnp.exp(draws), dims[axis_at] // blocks).reshape((-1,) + (1,) * (len(dims) - axis_at - 1))

    gain = one(*cuts[0])
    for cut in cuts[1:]:
        gain = gain * one(*cut)
    return gain


def scatter_about(own_key, extent, deviation, reach, cuts=(), dtype=jnp.bfloat16):
    values = deviation * jax.random.normal(own_key, extent, jnp.float32)
    if cuts:
        values = values * levels(own_key, extent, cuts, -0.22, 0.18)
    return jnp.clip(values, -reach, reach).astype(dtype)


def setup_inputs(seed: int = 0) -> dict:
    key_list = jax.random.split(jax.random.key(seed), 15)
    return {
        "feats": scatter_about(key_list[0], (FRAMES, ROWS, W, C), 1.0, 6.0, ((0, 4), (1, 8))),
        "conv_one": scatter_about(key_list[1], (3, 3, 3, C, C), (27 * C) ** -0.5, 0.078125),
        "bias_one": scatter_about(key_list[2], (C,), 0.5, 3.0, (), jnp.float32),
        "conv_two": scatter_about(key_list[3], (3, 3, 3, C, C), (27 * C) ** -0.5, 0.078125),
        "bias_two": scatter_about(key_list[4], (C,), 0.5, 3.0, (), jnp.float32),
        "patch_weight": scatter_about(key_list[5], (2, 2, C, LAT), (4 * C) ** -0.5, 0.1875),
        "patch_bias": scatter_about(key_list[6], (LAT,), 0.5, 3.0, (), jnp.float32),
        "embed_weight": scatter_about(key_list[7], (LAT, D), LAT ** -0.5, 0.5),
        "embed_bias": scatter_about(key_list[8], (D,), 1.0, 6.0, (), jnp.float32),
        "norm_gain": jnp.clip(1.0 + 0.18 * jax.random.normal(key_list[9], (D,), jnp.float32), 0.1, 1.9),
        "w_query": draw_w_query(jax.random.fold_in(key_list[14], 71), 0),
        "w_key": draw_w_key(jax.random.fold_in(key_list[14], 71), 0),
        "w_value": scatter_about(key_list[12], (D, D), D ** -0.5, 0.125, ((1, 8),)),
        "w_velocity": scatter_about(key_list[13], (D, LAT), (D // 16) ** -0.5, 0.5, ((0, 8),)),
    }


def convolve(field, kernel, bias):
    frames, rows, width, chans = field.shape
    padded = jnp.pad(field, ((1, 1), (1, 1), (1, 1), (0, 0)))
    total = jnp.zeros((frames * rows * width, kernel.shape[-1]), jnp.float32)
    for shift_t in range(3):
        for shift_r in range(3):
            window = padded[shift_t:shift_t + frames, shift_r:shift_r + rows]
            stacked = jnp.concatenate([window[:, :, shift_w:shift_w + width] for shift_w in range(3)], axis=-1)
            total = total + jnp.dot(stacked.reshape(-1, 3 * chans), kernel[shift_t, shift_r].reshape(3 * chans, -1), preferred_element_type=jnp.float32)
    return (total + bias).reshape(frames, rows, width, -1)

def patchify(field, weight, bias):
    frames, rows, width, chans = field.shape
    blocks = field.reshape(frames, rows // 2, 2, width // 2, 2, chans).transpose(0, 1, 3, 2, 4, 5).reshape(-1, 4 * chans)
    return (jnp.dot(blocks, weight.reshape(4 * chans, -1), preferred_element_type=jnp.float32) + bias).astype(jnp.bfloat16)

def normalize(latent_rows, embed_weight, embed_bias, norm_gain):
    hidden = jnp.dot(latent_rows, embed_weight, preferred_element_type=jnp.float32) + embed_bias
    center = hidden - hidden.mean(-1, keepdims=True)
    spread = (center * center).mean(-1, keepdims=True)
    return (center * lax.rsqrt(spread + 1e-05) * norm_gain).astype(jnp.bfloat16)

def head_attention(trio):
    query_head, key_head, value_head = trio
    scale = HEAD_DIM ** (-0.5)
    count = math.gcd(TOKENS, 1024)

    def one_block(query_block):
        scores = jnp.dot(query_block, key_head.T, preferred_element_type=jnp.float32) * scale
        probs = jnp.exp(scores - scores.max(-1, keepdims=True))
        denom = probs.sum(-1, keepdims=True)
        return (jnp.dot(probs.astype(jnp.bfloat16), value_head, preferred_element_type=jnp.float32) / denom).astype(jnp.bfloat16)
    return lax.map(one_block, query_head.reshape(-1, count, HEAD_DIM)).reshape(TOKENS, HEAD_DIM)

def reference(feats, conv_one, bias_one, conv_two, bias_two, patch_weight, patch_bias, embed_weight, embed_bias, norm_gain, w_query, w_key, w_value, w_velocity):
    first = jax.nn.gelu(convolve(feats, conv_one, bias_one), approximate=False).astype(jnp.bfloat16)
    second = (first.astype(jnp.float32) + jax.nn.gelu(convolve(first, conv_two, bias_two), approximate=False)).astype(jnp.bfloat16)
    patches = patchify(second, patch_weight, patch_bias)
    latents = patches.reshape(N_AA, FT, N_BA, SH // 2, W // 2, LAT).transpose(0, 2, 1, 3, 4, 5).reshape(TOKENS, LAT)
    normed = normalize(latents, embed_weight, embed_bias, norm_gain)
    queries = jnp.dot(normed, w_query, preferred_element_type=jnp.float32).astype(jnp.bfloat16)
    keys = jnp.dot(normed, w_key, preferred_element_type=jnp.float32).astype(jnp.bfloat16)
    values = jnp.dot(normed, w_value, preferred_element_type=jnp.float32).astype(jnp.bfloat16)

    def split_heads(matrix):
        return matrix.reshape(TOKENS, HEADS, HEAD_DIM).transpose(1, 0, 2)
    attended = lax.map(head_attention, (split_heads(queries), split_heads(keys), split_heads(values)))
    attended = attended.transpose(1, 0, 2).reshape(TOKENS, D)
    return jnp.dot(attended, w_velocity, preferred_element_type=jnp.float32)
```

```python
import functools
import math

import jax
import jax.numpy as jnp
from jax import lax
from jax.experimental import pallas as pl
from jax.experimental.pallas import tpu as pltpu
from jax.sharding import PartitionSpec as P

HEAD_DIM = 64
SLOT = 128
MESH = pl.DeviceIdType.MESH
F32 = jnp.float32
BF16 = jnp.bfloat16
VMEM_BYTES = 60 << 20
DIRECTIONS = ((0, -1), (0, 1), (-1, 0), (1, 0), (-1, -1), (-1, 1), (1, -1), (1, 1))


def dot(left, right):
    return jnp.dot(left, right, preferred_element_type=F32)


def two_parts(value):
    high = value.astype(BF16)
    return high, (value - high.astype(F32)).astype(BF16)


def gelu(value):
    return 0.5 * value * (1.0 + lax.erf(value * (0.5**0.5)))


def encode_kernel(
    n_aa, n_ba,
    feats, conv_one, bias_one, conv_two, bias_two, patch_weight, patch_bias,
    embed_weight, embed_bias, norm_gain, w_query, w_key, w_value,
    gathered, merged, gram,
    field_one, field_two, taps_one, taps_two, w_joined, acc, pair, load_sem,
    send_sem, recv_sem, aa_send, aa_recv, ba_send, ba_recv, core_send, core_recv,
):
    aa, ba = lax.axis_index("aa"), lax.axis_index("ba")
    _, rows, width, chans = feats.shape
    partner = ba + 1 - 2 * (ba % 2)
    half = n_ba // 2
    qwidth = w_query.shape[1]

    loads = [
        pltpu.make_async_copy(feats.at[0], field_one.at[1, pl.ds(1, rows)], load_sem.at[0]),
        pltpu.make_async_copy(conv_one, taps_one, load_sem.at[1]),
        pltpu.make_async_copy(w_query, w_joined.at[0], load_sem.at[2]),
        pltpu.make_async_copy(w_key, w_joined.at[1], load_sem.at[3]),
        pltpu.make_async_copy(w_value, w_joined.at[2], load_sem.at[4]),
        pltpu.make_async_copy(conv_two, taps_two, load_sem.at[5]),
    ]
    for load in loads:
        load.start()

    def there(da, db):
        inside = None
        if da == -1:
            inside = aa > 0
        if da == 1:
            inside = aa < n_aa - 1
        if db == -1:
            inside = ba > 0 if inside is None else jnp.logical_and(inside, ba > 0)
        if db == 1:
            last = ba < n_ba - 1
            inside = last if inside is None else jnp.logical_and(inside, last)
        return inside

    barrier = pltpu.get_barrier_semaphore()
    for da, db in DIRECTIONS:
        @pl.when(there(da, db))
        def _():
            pl.semaphore_signal(barrier, inc=1, device_id=(aa + da, ba + db), device_id_type=MESH)
    for step in range(1, n_aa):
        pl.semaphore_signal(
            barrier, inc=1, device_id=((aa + step) % n_aa, ba), device_id_type=MESH
        )
    for step in range(1, half):
        pl.semaphore_signal(
            barrier, inc=1, device_id=(aa, (ba + 2 * step) % n_ba), device_id_type=MESH
        )
    pl.semaphore_signal(barrier, inc=1, device_id=(aa, partner), device_id_type=MESH)

    def landing(field, da, db):
        row = slice(1, rows + 1) if db == 0 else (slice(0, 1) if db == 1 else slice(rows + 1, rows + 2))
        return field.at[1 - da, row]

    def halo(field, at):
        da, db = DIRECTIONS[at]
        row = slice(1, rows + 1) if db == 0 else (slice(rows, rows + 1) if db == 1 else slice(1, 2))
        return pltpu.make_async_remote_copy(
            src_ref=field.at[1, row],
            dst_ref=landing(field, da, db),
            send_sem=send_sem.at[0 if field is field_one else 1, at],
            recv_sem=recv_sem.at[0 if field is field_one else 1, at],
            device_id=(aa + da, ba + db),
            device_id_type=MESH,
        )

    def each(field, which, act):
        for at in which:
            da, db = DIRECTIONS[at]
            act(field, at, da, db)

    def send(field, at, da, db):
        @pl.when(there(da, db))
        def _():
            halo(field, at).start()

    def arrive(field, at, da, db):
        @pl.when(there(-da, -db))
        def _():
            halo(field, at).wait_recv()

    def sent(field, at, da, db):
        @pl.when(there(da, db))
        def _():
            halo(field, at).wait_send()

    def blank(field, at, da, db):
        @pl.when(jnp.logical_not(there(-da, -db)))
        def _():
            target = landing(field, da, db)
            target[...] = jnp.zeros(target.shape, target.dtype)

    neighbours = jnp.int32(n_aa - 1 + half - 1 + 1)
    for da, db in DIRECTIONS:
        neighbours = neighbours + there(da, db).astype(jnp.int32)
    every = range(8)
    each(field_one, every, blank)
    each(field_two, every, blank)
    pl.semaphore_wait(barrier, neighbours)
    loads[0].wait()
    each(field_one, every, send)

    embed = embed_weight[...].astype(F32)
    centred = jnp.concatenate(
        [
            embed - embed.mean(-1, keepdims=True),
            jnp.broadcast_to(
                embed_bias[...] - embed_bias[...].mean(-1, keepdims=True), (8, embed.shape[1])
            ),
        ],
        axis=0,
    )
    gram[...] = lax.dot_general(
        centred, centred, (((1,), (1,)), ((), ())),
        precision=lax.Precision.HIGHEST, preferred_element_type=F32,
    ) * (1.0 / embed.shape[1])
    gained_high, gained_low = two_parts(centred * norm_gain[...])
    for which in range(3):
        loads[2 + which].wait()
        product = dot(gained_high, w_joined[which]) + dot(gained_low, w_joined[which])
        if which == 0:
            product = product * (HEAD_DIM**-0.5 * math.log2(math.e))
        blanks = jnp.zeros((product.shape[0], SLOT - HEAD_DIM), F32)
        for head in range(qwidth // HEAD_DIM):
            piece = product[:, head * HEAD_DIM : (head + 1) * HEAD_DIM]
            merged[which, :, head * SLOT : (head + 1) * SLOT] = jnp.concatenate(
                [piece, blanks], axis=1
            )

    def convolve(field, taps, bias):
        def tap(shift_t, shift_r, first):
            window = field[shift_t, pl.ds(shift_r, rows)].reshape(rows * width, chans)
            for shift_w in range(3):
                part = dot(window, taps[(shift_t * 3 + shift_r) * 3 + shift_w])
                if first:
                    acc[shift_w] = part
                else:
                    acc[shift_w] += part

        tap(1, 1, True)
        each(field, (0, 1), arrive)
        tap(1, 0, False)
        tap(1, 2, False)
        each(field, (2, 3), arrive)
        tap(0, 1, False)
        tap(2, 1, False)
        each(field, (4, 5, 6, 7), arrive)

        @pl.loop(0, 2)
        def _(index):
            tap(0, 2 * index, False)
            tap(2, 2 * index, False)

        total = acc[1] + bias
        place = lax.broadcasted_iota(jnp.int32, total.shape, 0) % width
        total += jnp.where(place == 0, 0.0, pltpu.roll(acc[0], 1, 0))
        total += jnp.where(place == width - 1, 0.0, pltpu.roll(acc[2], rows * width - 1, 0))
        return total

    loads[1].wait()
    first = gelu(convolve(field_one, taps_one, bias_one[...])).astype(BF16)
    field_two[1, 1 : rows + 1] = first.reshape(rows, width, chans)
    each(field_two, every, send)
    loads[5].wait()
    total = convolve(field_two, taps_two, bias_two[...])
    own = field_two[1, 1 : rows + 1].reshape(rows * width, chans).astype(F32)
    second = (own + gelu(total)).astype(BF16)

    tokens = rows * width // 4
    line = width // 2
    for block in range(rows // 2):
        upper = second[(2 * block) * width : (2 * block + 1) * width]
        lower = second[(2 * block + 1) * width : (2 * block + 2) * width]
        for col in range(2):
            pair[col] = dot(upper, patch_weight[0, col]) + dot(lower, patch_weight[1, col])
        patches = (
            pair[0, pl.ds(0, line, stride=2), :] + pair[1, pl.ds(1, line, stride=2), :]
            + patch_bias[...]
        ).astype(BF16)
        gathered[ba, pl.ds(pl.multiple_of(aa * tokens + block * line, line), line), :] = patches

    def along_aa(step):
        block = gathered.at[ba, pl.ds(pl.multiple_of(aa * tokens, tokens), tokens)]
        return pltpu.make_async_remote_copy(
            src_ref=block, dst_ref=block, send_sem=aa_send.at[step], recv_sem=aa_recv.at[step],
            device_id=((aa + step) % n_aa, ba), device_id_type=MESH,
        )

    def along_ba(step):
        return pltpu.make_async_remote_copy(
            src_ref=gathered.at[ba], dst_ref=gathered.at[ba],
            send_sem=ba_send.at[step], recv_sem=ba_recv.at[step],
            device_id=(aa, (ba + 2 * step) % n_ba), device_id_type=MESH,
        )

    def to_partner(step):
        block = gathered.at[(ba + n_ba - 2 * step) % n_ba]
        return pltpu.make_async_remote_copy(
            src_ref=block, dst_ref=block, send_sem=core_send.at[step], recv_sem=core_recv.at[step],
            device_id=(aa, partner), device_id_type=MESH,
        )

    for step in range(1, n_aa):
        along_aa(step).start()
    each(field_one, every, sent)
    each(field_two, every, sent)
    for step in range(1, n_aa):
        along_aa(step).wait_recv()
    for step in range(1, half):
        along_ba(step).start()
    to_partner(0).start()
    for step in range(1, half):
        along_ba(step).wait_recv()
        to_partner(step).start()
    for step in range(half):
        to_partner(step).wait_recv()
    for step in range(1, n_aa):
        along_aa(step).wait_send()
    for step in range(1, half):
        along_ba(step).wait_send()
    for step in range(half):
        to_partner(step).wait_send()


def attend_kernel(
    n_aa, n_ba, span, chunk,
    gathered, merged, gram, w_velocity, out,
    queries, keys, values, split, shares, arrived, send_sem, recv_sem,
):
    aa, ba = lax.axis_index("aa"), lax.axis_index("ba")
    heads = w_velocity.shape[0] // HEAD_DIM
    count = gathered.shape[1] // n_aa
    lat = gathered.shape[2]
    per_span = span // count

    barrier = pltpu.get_barrier_semaphore()
    for step in range(1, n_ba):
        pl.semaphore_signal(
            barrier, inc=1, device_id=(aa, (ba + step) % n_ba), device_id_type=MESH
        )

    for which in range(3):
        high, low = two_parts(merged[which, :lat])
        split[which, 0] = high
        split[which, 1] = low
    gram_high, gram_low = two_parts(gram[:lat, :lat])
    slope = 2.0 * gram[lat : lat + 1, :lat]
    floor = gram[lat : lat + 1, lat : lat + 1]

    def spread_of(latents):
        bent = dot(latents, gram_high) + dot(latents, gram_low) + slope
        power = (bent * latents.astype(F32)).sum(-1, keepdims=True) + floor
        return lax.rsqrt(jnp.maximum(power, 0.0) + 1e-05)

    def project(latents, scale, which):
        flat = dot(latents, split[which, 0]) + dot(latents, split[which, 1])
        return ((flat + merged[which, lat : lat + 1]) * scale).astype(BF16)

    column = lax.broadcasted_iota(jnp.int32, (gathered.shape[1], SLOT), 1)

    @pl.loop(0, n_ba)
    def _(block):
        latents = gathered[block]
        scale = spread_of(latents)
        projected_keys = project(latents, scale, 1)
        projected_values = project(latents, scale, 2)
        where = pl.ds(pl.multiple_of(block * latents.shape[0], latents.shape[0]), latents.shape[0])
        for head in range(heads):
            keys[head, where] = projected_keys[:, head * SLOT : (head + 1) * SLOT]
            values[head, where] = jnp.where(
                column == HEAD_DIM,
                jnp.ones((), BF16),
                projected_values[:, head * SLOT : (head + 1) * SLOT],
            )
        mine = gathered[block, pl.ds(pl.multiple_of(aa * count, count), count)]
        asked = project(mine, spread_of(mine), 0)
        there = pl.ds(pl.multiple_of(block * count, count), count)
        for head in range(heads):
            queries[head, there] = asked[:, head * SLOT : (head + 1) * SLOT]

    pl.semaphore_wait(barrier, n_ba - 1)

    def share(dest):
        offset = (dest + n_ba - ba) % n_ba
        return pltpu.make_async_remote_copy(
            src_ref=shares.at[dest], dst_ref=arrived.at[ba],
            send_sem=send_sem.at[offset], recv_sem=recv_sem.at[offset],
            device_id=(aa, dest), device_id_type=MESH,
        )

    spans = n_ba // per_span
    total = keys.shape[1]
    big = math.gcd(total, 4096)

    @pl.loop(0, spans)
    def _(step):
        at = (ba // per_span + 1 + step) % spans
        where = pl.ds(pl.multiple_of(at * span, span), span)

        def one_head(head, velocity):
            asked = queries[head, where]

            def one_big(index, state):
                best, accum = state
                for piece in range(big // chunk):
                    held = pl.ds(pl.multiple_of(index * big + piece * chunk, chunk), chunk)
                    scores = lax.dot_general(
                        asked, keys[head, held], (((1,), (1,)), ((), ())),
                        preferred_element_type=F32,
                    )
                    peak = jnp.maximum(best, scores.max(-1, keepdims=True))
                    probs = jnp.exp2(scores - peak).astype(BF16)
                    accum = accum * jnp.exp2(best - peak) + dot(probs, values[head, held])
                    best = peak
                return best, accum

            state = (jnp.full((span, 1), -jnp.inf, F32), jnp.zeros((span, SLOT), F32))
            if total == big:
                _, accum = one_big(0, state)
            else:
                _, accum = lax.fori_loop(0, total // big, one_big, state)
            attended = (accum[:, :HEAD_DIM] / accum[:, HEAD_DIM : HEAD_DIM + 1]).astype(BF16)
            rows = pl.ds(pl.multiple_of(head * HEAD_DIM, HEAD_DIM), HEAD_DIM)
            return velocity + dot(attended, w_velocity[rows])

        velocity = lax.fori_loop(0, heads, one_head, jnp.zeros((span, w_velocity.shape[1]), F32))
        for part in range(per_span):
            dest = at * per_span + part
            shares[dest] = velocity[part * count : (part + 1) * count].astype(BF16)

            @pl.when(dest != ba)
            def _():
                share(dest).start()

    summed = shares[ba].astype(F32)
    for offset in range(1, n_ba):
        share((ba + offset) % n_ba).wait_recv()
        summed += arrived[(ba + n_ba - offset) % n_ba].astype(F32)
    out[...] = summed
    for offset in range(1, n_ba):
        share((ba + offset) % n_ba).wait_send()


def on_device(
    n_aa, n_ba,
    feats, conv_one, bias_one, conv_two, bias_two, patch_weight, patch_bias,
    embed_weight, embed_bias, norm_gain, w_query, w_key, w_value, w_velocity,
):
    _, rows, width, chans = feats.shape
    lat = patch_bias.shape[0]
    features, qwidth = w_query.shape
    heads = qwidth // HEAD_DIM
    tokens = rows * width // 4
    vmem = pl.BlockSpec(memory_space=pltpu.VMEM)
    anywhere = pl.BlockSpec(memory_space=pl.ANY)
    dma = pltpu.SemaphoreType.DMA
    gathered, merged, gram = pl.pallas_call(
        functools.partial(encode_kernel, n_aa, n_ba),
        out_shape=(
            jax.ShapeDtypeStruct((n_ba, n_aa * tokens, lat), BF16),
            jax.ShapeDtypeStruct((3, lat + 8, heads * SLOT), F32),
            jax.ShapeDtypeStruct((lat + 8, lat + 8), F32),
        ),
        in_specs=[anywhere, anywhere, vmem, anywhere] + [vmem] * 6 + [anywhere] * 3,
        out_specs=(vmem, vmem, vmem),
        scratch_shapes=[
            pltpu.VMEM((3, rows + 2, width, chans), BF16),
            pltpu.VMEM((3, rows + 2, width, chans), BF16),
            pltpu.VMEM((27, chans, chans), BF16),
            pltpu.VMEM((27, chans, chans), BF16),
            pltpu.VMEM((3, features, qwidth), BF16),
            pltpu.VMEM((3, rows * width, chans), F32),
            pltpu.VMEM((2, width, lat), F32),
            dma((6,)), dma((2, 8)), dma((2, 8)),
            dma((n_aa,)), dma((n_aa,)),
            dma((n_ba // 2,)), dma((n_ba // 2,)),
            dma((n_ba // 2,)), dma((n_ba // 2,)),
        ],
        compiler_params=pltpu.CompilerParams(
            collective_id=0, has_side_effects=True, vmem_limit_bytes=VMEM_BYTES
        ),
        name="encode",
    )(
        feats, conv_one.reshape(27, chans, chans), bias_one[None],
        conv_two.reshape(27, chans, chans), bias_two[None],
        patch_weight, patch_bias[None], embed_weight, embed_bias[None], norm_gain[None],
        w_query, w_key, w_value,
    )
    total = n_ba * n_aa * tokens
    span = max(tokens, min(256, n_ba * tokens))
    chunk = math.gcd(total, 1024)
    return pl.pallas_call(
        functools.partial(attend_kernel, n_aa, n_ba, span, chunk),
        out_shape=jax.ShapeDtypeStruct((tokens, lat), F32),
        in_specs=[vmem] * 4,
        out_specs=vmem,
        scratch_shapes=[
            pltpu.VMEM((heads, n_ba * tokens, SLOT), BF16),
            pltpu.VMEM((heads, total, SLOT), BF16),
            pltpu.VMEM((heads, total, SLOT), BF16),
            pltpu.VMEM((3, 2, lat, heads * SLOT), BF16),
            pltpu.VMEM((n_ba, tokens, lat), BF16),
            pltpu.VMEM((n_ba, tokens, lat), BF16),
            dma((n_ba,)), dma((n_ba,)),
        ],
        compiler_params=pltpu.CompilerParams(
            collective_id=1, has_side_effects=True, vmem_limit_bytes=VMEM_BYTES
        ),
        name="attend",
    )(gathered, merged, gram, w_velocity)


def solution(mesh):
    return jax.shard_map(
        functools.partial(on_device, mesh.shape["aa"], mesh.shape["ba"]),
        mesh=mesh,
        in_specs=(
            P("aa", "ba", None, None), P(), P(), P(), P(), P(), P(), P(), P(), P(),
            P(None, "ba"), P(None, "ba"), P(None, "ba"), P("ba", None),
        ),
        out_specs=P(("aa", "ba"), None),
        check_vma=False,
    )
```

```python
import functools
import math

import jax
import jax.numpy as jnp
from jax import lax
from jax.experimental import pallas as pl
from jax.experimental.pallas import tpu as pltpu
from jax.sharding import PartitionSpec as P

HEAD_DIM = 64
SLOT = 128
MESH = pl.DeviceIdType.MESH
F32 = jnp.float32
BF16 = jnp.bfloat16
VMEM_BYTES = 67043328


def dot(left, right):
    return jnp.dot(left, right, preferred_element_type=F32)


def two_parts(value):
    high = value.astype(BF16)
    return high, (value - high.astype(F32)).astype(BF16)


def gelu(value):
    return 0.5 * value * (1.0 + lax.erf(value * (0.5**0.5)))


def whole_kernel(
    n_aa, n_ba, span, chunk,
    feats, conv_one, bias_one, conv_two, bias_two, patch_weight, patch_bias,
    embed_weight, embed_bias, norm_gain, w_query, w_key, w_value, w_velocity,
    out,
    field_one, field_two, taps, w_joined, acc, pair, gathered, split, offsets, gram_split, gram,
    queries, keys, values, shares, arrived,
    load_sem, aa_side_send, aa_side_recv, ba_side_send, ba_side_recv,
    aa_send, aa_recv, ba_send, ba_recv, core_send, core_recv, share_send, share_recv,
):
    aa, ba = lax.axis_index("aa"), lax.axis_index("ba")
    _, rows, width, chans = feats.shape
    partner = ba + 1 - 2 * (ba % 2)
    half = n_ba // 2
    heads = w_query.shape[1] // HEAD_DIM
    tokens = rows * width // 4
    lat = patch_bias.shape[1]

    def load(source, target, at):
        return pltpu.make_async_copy(source, target, load_sem.at[at])

    loads = [
        load(feats.at[0], field_one.at[1, pl.ds(1, rows)], 0),
        load(conv_one, taps, 1),
        load(w_query, w_joined.at[0], 2),
        load(w_key, w_joined.at[1], 3),
        load(w_value, w_joined.at[2], 4),
    ]
    for one in loads:
        one.start()

    def aa_there(side):
        return aa > 0 if side == -1 else aa < n_aa - 1

    def ba_there(side):
        return ba > 0 if side == -1 else ba < n_ba - 1

    barrier = pltpu.get_barrier_semaphore()
    for step in range(1, n_aa):
        pl.semaphore_signal(
            barrier, inc=1, device_id=((aa + step) % n_aa, ba), device_id_type=MESH
        )
    for step in range(1, n_ba):
        pl.semaphore_signal(
            barrier, inc=1, device_id=(aa, (ba + step) % n_ba), device_id_type=MESH
        )

    def along_time(field, side, piece):
        row = (slice(1, 2), slice(rows, rows + 1), slice(2, rows))[piece]
        at = (0 if field is field_one else 1, (side + 1) // 2, piece)
        return pltpu.make_async_remote_copy(
            src_ref=field.at[1, row], dst_ref=field.at[1 - side, row],
            send_sem=aa_side_send.at[at], recv_sem=aa_side_recv.at[at],
            device_id=(aa + side, ba), device_id_type=MESH,
        )

    def along_rows(field, frame, side):
        source, target = (rows, 0) if side == 1 else (1, rows + 1)
        at = (0 if field is field_one else 1, frame, (side + 1) // 2)
        return pltpu.make_async_remote_copy(
            src_ref=field.at[frame, pl.ds(source, 1)], dst_ref=field.at[frame, pl.ds(target, 1)],
            send_sem=ba_side_send.at[at], recv_sem=ba_side_recv.at[at],
            device_id=(aa, ba + side), device_id_type=MESH,
        )

    def send_field(field):
        for side in (-1, 1):
            pl.when(ba_there(side))(along_rows(field, 1, side).start)
        for piece in range(3):
            for side in (-1, 1):
                pl.when(aa_there(side))(along_time(field, side, piece).start)

    def take_time(field, pieces):
        for side in (-1, 1):
            @pl.when(aa_there(-side))
            def _():
                for piece in pieces:
                    along_time(field, side, piece).wait_recv()

    def relay_rows(field):
        for frame, behind in ((0, -1), (2, 1)):
            for side in (-1, 1):
                pl.when(jnp.logical_and(aa_there(behind), ba_there(side)))(
                    along_rows(field, frame, side).start
                )

    def take_rows(field, frame):
        for side in (-1, 1):
            inside = ba_there(-side)
            if frame != 1:
                inside = jnp.logical_and(inside, aa_there(frame - 1))
            pl.when(inside)(along_rows(field, frame, side).wait_recv)

    def sent(field):
        for side in (-1, 1):
            @pl.when(aa_there(side))
            def _():
                for piece in range(3):
                    along_time(field, side, piece).wait_send()

            pl.when(ba_there(side))(along_rows(field, 1, side).wait_send)
            for frame, behind in ((0, -1), (2, 1)):
                pl.when(jnp.logical_and(aa_there(behind), ba_there(side)))(
                    along_rows(field, frame, side).wait_send
                )

    def blank(field):
        line = jnp.zeros((width, chans), BF16)
        for frame, behind in ((0, -1), (2, 1)):
            @pl.when(jnp.logical_not(aa_there(behind)))
            def _():
                for row in range(rows + 2):
                    field[frame, row] = line

            @pl.when(aa_there(behind))
            def _():
                for side, row in ((-1, 0), (1, rows + 1)):
                    @pl.when(jnp.logical_not(ba_there(side)))
                    def _():
                        field[frame, row] = line
        for side, row in ((-1, 0), (1, rows + 1)):
            @pl.when(jnp.logical_not(ba_there(side)))
            def _():
                field[1, row] = line

    blank(field_one)
    blank(field_two)
    pl.semaphore_wait(barrier, n_aa - 1 + n_ba - 1)
    loads[0].wait()
    send_field(field_one)

    def merge_weights():
        embed = embed_weight[...].astype(F32)
        centred = jnp.concatenate(
            [
                embed - embed.mean(-1, keepdims=True),
                jnp.broadcast_to(
                    embed_bias[...] - embed_bias[...].mean(-1, keepdims=True),
                    (8, embed.shape[1]),
                ),
            ],
            axis=0,
        )
        gram[...] = lax.dot_general(
            centred, centred, (((1,), (1,)), ((), ())),
            precision=lax.Precision.HIGHEST, preferred_element_type=F32,
        ) * (1.0 / embed.shape[1])
        high, low = two_parts(gram[:lat, :lat])
        gram_split[:lat] = high
        gram_split[lat:] = low
        gained_high, gained_low = two_parts(centred * norm_gain[...])
        for which in range(3):
            loads[2 + which].wait()
            product = dot(gained_high, w_joined[which]) + dot(gained_low, w_joined[which])
            if which == 0:
                product = product * (HEAD_DIM**-0.5 * math.log2(math.e))
            blanks = jnp.zeros((product.shape[0], SLOT - HEAD_DIM), F32)
            for head in range(heads):
                piece = jnp.concatenate(
                    [product[:, head * HEAD_DIM : (head + 1) * HEAD_DIM], blanks], axis=1
                )
                slot = slice(head * SLOT, (head + 1) * SLOT)
                high, low = two_parts(piece[:lat])
                split[which, :lat, slot] = high
                split[which, lat:, slot] = low
                offsets[which, :, slot] = piece[lat:]

    def convolve(field, bias, filler):
        def tap(shift_t, shift_r, first):
            window = field[shift_t, pl.ds(shift_r, rows)].reshape(rows * width, chans)
            for shift_w in range(3):
                part = dot(window, taps[(shift_t * 3 + shift_r) * 3 + shift_w])
                if first:
                    acc[shift_w] = part
                else:
                    acc[shift_w] += part

        tap(1, 1, True)
        take_rows(field, 1)
        tap(1, 0, False)
        tap(1, 2, False)
        take_time(field, (0, 1))
        relay_rows(field)
        filler()
        take_time(field, (2,))
        tap(0, 1, False)
        tap(2, 1, False)
        take_rows(field, 0)
        take_rows(field, 2)

        @pl.loop(0, 2)
        def _(index):
            tap(0, 2 * index, False)
            tap(2, 2 * index, False)

        total = acc[1] + bias
        place = lax.broadcasted_iota(jnp.int32, total.shape, 0) % width
        total += jnp.where(place == 0, 0.0, pltpu.roll(acc[0], 1, 0))
        total += jnp.where(place == width - 1, 0.0, pltpu.roll(acc[2], rows * width - 1, 0))
        return total

    loads[1].wait()
    first = gelu(convolve(field_one, bias_one[...], merge_weights)).astype(BF16)
    field_two[1, 1 : rows + 1] = first.reshape(rows, width, chans)
    send_field(field_two)
    again = load(conv_two, taps, 5)
    again.start()
    again.wait()
    total = convolve(field_two, bias_two[...], lambda: None)
    own = field_two[1, 1 : rows + 1].reshape(rows * width, chans).astype(F32)
    second = (own + gelu(total)).astype(BF16)

    line = width // 2
    for block in range(rows // 2):
        upper = second[(2 * block) * width : (2 * block + 1) * width]
        lower = second[(2 * block + 1) * width : (2 * block + 2) * width]
        for col in range(2):
            pair[col] = dot(upper, patch_weight[0, col]) + dot(lower, patch_weight[1, col])
        patches = (
            pair[0, pl.ds(0, line, stride=2), :] + pair[1, pl.ds(1, line, stride=2), :]
            + patch_bias[...]
        ).astype(BF16)
        gathered[ba, pl.ds(pl.multiple_of(aa * tokens + block * line, line), line), :] = patches

    def along_aa(step):
        block = gathered.at[ba, pl.ds(pl.multiple_of(aa * tokens, tokens), tokens)]
        return pltpu.make_async_remote_copy(
            src_ref=block, dst_ref=block, send_sem=aa_send.at[step], recv_sem=aa_recv.at[step],
            device_id=((aa + step) % n_aa, ba), device_id_type=MESH,
        )

    def along_ba(step):
        return pltpu.make_async_remote_copy(
            src_ref=gathered.at[ba], dst_ref=gathered.at[ba],
            send_sem=ba_send.at[step], recv_sem=ba_recv.at[step],
            device_id=(aa, (ba + 2 * step) % n_ba), device_id_type=MESH,
        )

    def to_partner(step):
        block = gathered.at[(ba + n_ba - 2 * step) % n_ba]
        return pltpu.make_async_remote_copy(
            src_ref=block, dst_ref=block, send_sem=core_send.at[step], recv_sem=core_recv.at[step],
            device_id=(aa, partner), device_id_type=MESH,
        )

    slope = 2.0 * gram[lat : lat + 1, :lat]
    floor = gram[lat : lat + 1, lat : lat + 1]
    column = lax.broadcasted_iota(jnp.int32, (n_aa * tokens, SLOT), 1)

    def spread_of(latents, twice):
        bent = dot(twice, gram_split[...]) + slope
        power = (bent * latents.astype(F32)).sum(-1, keepdims=True) + floor
        return lax.rsqrt(jnp.maximum(power, 0.0) + 1e-05)

    def project(twice, scale, which):
        return ((dot(twice, split[which]) + offsets[which, :1]) * scale).astype(BF16)

    def take_block(block):
        latents = gathered[block]
        twice = jnp.concatenate([latents, latents], axis=1)
        scale = spread_of(latents, twice)
        projected_keys = project(twice, scale, 1)
        projected_values = project(twice, scale, 2)
        length = n_aa * tokens
        where = pl.ds(pl.multiple_of(block * length, length), length)
        for head in range(heads):
            keys[head, where] = projected_keys[:, head * SLOT : (head + 1) * SLOT]
            values[head, where] = jnp.where(
                column == HEAD_DIM,
                jnp.ones((), BF16),
                projected_values[:, head * SLOT : (head + 1) * SLOT],
            )
        mine = gathered[block, pl.ds(pl.multiple_of(aa * tokens, tokens), tokens)]
        twice = jnp.concatenate([mine, mine], axis=1)
        asked = project(twice, spread_of(mine, twice), 0)
        there = pl.ds(pl.multiple_of(block * tokens, tokens), tokens)
        for head in range(heads):
            queries[head, there] = asked[:, head * SLOT : (head + 1) * SLOT]

    for step in range(1, n_aa):
        along_aa(step).start()
    sent(field_one)
    sent(field_two)
    for step in range(1, n_aa):
        along_aa(step).wait_recv()
    for step in range(1, half):
        along_ba(step).start()
    to_partner(0).start()
    take_block(ba)
    to_partner(0).wait_recv()
    take_block(partner)

    @pl.loop(1, half)
    def _(step):
        along_ba(step).wait_recv()
        to_partner(step).start()
        take_block((ba + n_ba - 2 * step) % n_ba)

    @pl.loop(1, half)
    def _(step):
        to_partner(step).wait_recv()
        take_block((partner + n_ba - 2 * step) % n_ba)

    for step in range(1, n_aa):
        along_aa(step).wait_send()
    for step in range(1, half):
        along_ba(step).wait_send()
    for step in range(half):
        to_partner(step).wait_send()

    def share(dest):
        offset = (dest + n_ba - ba) % n_ba
        return pltpu.make_async_remote_copy(
            src_ref=shares.at[dest], dst_ref=arrived.at[ba],
            send_sem=share_send.at[offset], recv_sem=share_recv.at[offset],
            device_id=(aa, dest), device_id_type=MESH,
        )

    per_span = span // tokens
    spans = n_ba // per_span
    total = keys.shape[1]
    big = math.gcd(total, 4096)

    @pl.loop(0, spans)
    def _(step):
        at = (ba // per_span + 1 + step) % spans
        where = pl.ds(pl.multiple_of(at * span, span), span)

        def one_head(head, velocity):
            asked = queries[head, where]

            def one_big(index, state):
                best, accum = state
                for piece in range(big // chunk):
                    held = pl.ds(pl.multiple_of(index * big + piece * chunk, chunk), chunk)
                    scores = lax.dot_general(
                        asked, keys[head, held], (((1,), (1,)), ((), ())),
                        preferred_element_type=F32,
                    )
                    peak = jnp.maximum(best, scores.max(-1, keepdims=True))
                    probs = jnp.exp2(scores - peak).astype(BF16)
                    accum = accum * jnp.exp2(best - peak) + dot(probs, values[head, held])
                    best = peak
                return best, accum

            state = (jnp.full((span, 1), -jnp.inf, F32), jnp.zeros((span, SLOT), F32))
            if total == big:
                _, accum = one_big(0, state)
            else:
                _, accum = lax.fori_loop(0, total // big, one_big, state)
            attended = (accum[:, :HEAD_DIM] / accum[:, HEAD_DIM : HEAD_DIM + 1]).astype(BF16)
            rows = pl.ds(pl.multiple_of(head * HEAD_DIM, HEAD_DIM), HEAD_DIM)
            return velocity + dot(attended, w_velocity[rows])

        velocity = lax.fori_loop(0, heads, one_head, jnp.zeros((span, w_velocity.shape[1]), F32))
        for part in range(per_span):
            dest = at * per_span + part
            shares[dest] = velocity[part * tokens : (part + 1) * tokens].astype(BF16)

            @pl.when(dest != ba)
            def _():
                share(dest).start()

    summed = shares[ba].astype(F32)
    for offset in range(1, n_ba):
        share((ba + offset) % n_ba).wait_recv()
        summed += arrived[(ba + n_ba - offset) % n_ba].astype(F32)
    out[...] = summed
    for offset in range(1, n_ba):
        share((ba + offset) % n_ba).wait_send()


def on_device(
    n_aa, n_ba,
    feats, conv_one, bias_one, conv_two, bias_two, patch_weight, patch_bias,
    embed_weight, embed_bias, norm_gain, w_query, w_key, w_value, w_velocity,
):
    _, rows, width, chans = feats.shape
    lat = patch_bias.shape[0]
    features, qwidth = w_query.shape
    heads = qwidth // HEAD_DIM
    tokens = rows * width // 4
    total = n_ba * n_aa * tokens
    span = max(tokens, min(512, n_ba * tokens))
    chunk = math.gcd(total, 2048)
    vmem = pl.BlockSpec(memory_space=pltpu.VMEM)
    anywhere = pl.BlockSpec(memory_space=pl.ANY)
    dma = pltpu.SemaphoreType.DMA
    return pl.pallas_call(
        functools.partial(whole_kernel, n_aa, n_ba, span, chunk),
        out_shape=jax.ShapeDtypeStruct((tokens, lat), F32),
        in_specs=[anywhere, anywhere, vmem, anywhere] + [vmem] * 6 + [anywhere] * 3 + [vmem],
        out_specs=vmem,
        scratch_shapes=[
            pltpu.VMEM((3, rows + 2, width, chans), BF16),
            pltpu.VMEM((3, rows + 2, width, chans), BF16),
            pltpu.VMEM((27, chans, chans), BF16),
            pltpu.VMEM((3, features, qwidth), BF16),
            pltpu.VMEM((3, rows * width, chans), F32),
            pltpu.VMEM((2, width, lat), F32),
            pltpu.VMEM((n_ba, n_aa * tokens, lat), BF16),
            pltpu.VMEM((3, 2 * lat, heads * SLOT), BF16),
            pltpu.VMEM((3, 8, heads * SLOT), F32),
            pltpu.VMEM((2 * lat, lat), BF16),
            pltpu.VMEM((lat + 8, lat + 8), F32),
            pltpu.VMEM((heads, n_ba * tokens, SLOT), BF16),
            pltpu.VMEM((heads, total, SLOT), BF16),
            pltpu.VMEM((heads, total, SLOT), BF16),
            pltpu.VMEM((n_ba, tokens, lat), BF16),
            pltpu.VMEM((n_ba, tokens, lat), BF16),
            dma((6,)),
            dma((2, 2, 3)), dma((2, 2, 3)), dma((2, 3, 2)), dma((2, 3, 2)),
            dma((n_aa,)), dma((n_aa,)),
            dma((n_ba // 2,)), dma((n_ba // 2,)),
            dma((n_ba // 2,)), dma((n_ba // 2,)),
            dma((n_ba,)), dma((n_ba,)),
        ],
        compiler_params=pltpu.CompilerParams(
            collective_id=0, has_side_effects=True, vmem_limit_bytes=VMEM_BYTES
        ),
        name="whole",
    )(
        feats, conv_one.reshape(27, chans, chans), bias_one[None],
        conv_two.reshape(27, chans, chans), bias_two[None],
        patch_weight, patch_bias[None], embed_weight, embed_bias[None], norm_gain[None],
        w_query, w_key, w_value, w_velocity,
    )


def solution(mesh):
    return jax.shard_map(
        functools.partial(on_device, mesh.shape["aa"], mesh.shape["ba"]),
        mesh=mesh,
        in_specs=(
            P("aa", "ba", None, None), P(), P(), P(), P(), P(), P(), P(), P(), P(),
            P(None, "ba"), P(None, "ba"), P(None, "ba"), P("ba", None),
        ),
        out_specs=P(("aa", "ba"), None),
        check_vma=False,
    )
```

```python
import functools
import math

import jax
import jax.numpy as jnp
from jax import lax
from jax.experimental import pallas as pl
from jax.experimental.pallas import tpu as pltpu
from jax.sharding import PartitionSpec as P

HEAD_DIM = 64
SLOT = 128
MESH = pl.DeviceIdType.MESH
F32 = jnp.float32
BF16 = jnp.bfloat16
VMEM_BYTES = 67043328


def dot(left, right):
    return jnp.dot(left, right, preferred_element_type=F32)


def two_parts(value):
    high = value.astype(BF16)
    return high, (value - high.astype(F32)).astype(BF16)


def gelu(value):
    return 0.5 * value * (1.0 + lax.erf(value * (0.5**0.5)))


def whole_kernel(
    n_aa, n_ba, span, chunk,
    feats, conv_one, bias_one, conv_two, bias_two, patch_weight, patch_bias,
    embed_weight, embed_bias, norm_gain, w_query, w_key, w_value, w_velocity,
    out,
    field_one, field_two, taps, w_joined, acc, pair, gathered, split, offsets, gram_split, gram,
    queries, keys, values, shares, arrived,
    load_sem, aa_side_send, aa_side_recv, ba_side_send, ba_side_recv,
    aa_send, aa_recv, ba_send, ba_recv, core_send, core_recv, share_send, share_recv,
):
    aa, ba = lax.axis_index("aa"), lax.axis_index("ba")
    _, rows, width, chans = feats.shape
    partner = ba + 1 - 2 * (ba % 2)
    half = n_ba // 2
    heads = w_query.shape[1] // HEAD_DIM
    tokens = rows * width // 4
    lat = patch_bias.shape[1]

    def load(source, target, at):
        return pltpu.make_async_copy(source, target, load_sem.at[at])

    loads = [
        load(feats.at[0], field_one.at[1, pl.ds(1, rows)], 0),
        load(conv_one, taps, 1),
        load(w_query, w_joined.at[0], 2),
        load(w_key, w_joined.at[1], 3),
        load(w_value, w_joined.at[2], 4),
    ]
    for one in loads:
        one.start()

    def aa_there(side):
        return aa > 0 if side == -1 else aa < n_aa - 1

    def ba_there(side):
        return ba > 0 if side == -1 else ba < n_ba - 1

    barrier = pltpu.get_barrier_semaphore()
    for step in range(1, n_aa):
        pl.semaphore_signal(
            barrier, inc=1, device_id=((aa + step) % n_aa, ba), device_id_type=MESH
        )
    for step in range(1, n_ba):
        pl.semaphore_signal(
            barrier, inc=1, device_id=(aa, (ba + step) % n_ba), device_id_type=MESH
        )

    def along_time(field, side, piece):
        row = (slice(1, 2), slice(rows, rows + 1), slice(2, rows))[piece]
        at = (0 if field is field_one else 1, (side + 1) // 2, piece)
        return pltpu.make_async_remote_copy(
            src_ref=field.at[1, row], dst_ref=field.at[1 - side, row],
            send_sem=aa_side_send.at[at], recv_sem=aa_side_recv.at[at],
            device_id=(aa + side, ba), device_id_type=MESH,
        )

    def along_rows(field, frame, side):
        source, target = (rows, 0) if side == 1 else (1, rows + 1)
        at = (0 if field is field_one else 1, frame, (side + 1) // 2)
        return pltpu.make_async_remote_copy(
            src_ref=field.at[frame, pl.ds(source, 1)], dst_ref=field.at[frame, pl.ds(target, 1)],
            send_sem=ba_side_send.at[at], recv_sem=ba_side_recv.at[at],
            device_id=(aa, ba + side), device_id_type=MESH,
        )

    def send_field(field):
        for side in (-1, 1):
            pl.when(ba_there(side))(along_rows(field, 1, side).start)
        for piece in range(3):
            for side in (-1, 1):
                pl.when(aa_there(side))(along_time(field, side, piece).start)

    def take_time(field, pieces):
        for side in (-1, 1):
            @pl.when(aa_there(-side))
            def _():
                for piece in pieces:
                    along_time(field, side, piece).wait_recv()

    def relay_rows(field):
        for frame, behind in ((0, -1), (2, 1)):
            for side in (-1, 1):
                pl.when(jnp.logical_and(aa_there(behind), ba_there(side)))(
                    along_rows(field, frame, side).start
                )

    def take_rows(field, frame):
        for side in (-1, 1):
            inside = ba_there(-side)
            if frame != 1:
                inside = jnp.logical_and(inside, aa_there(frame - 1))
            pl.when(inside)(along_rows(field, frame, side).wait_recv)

    def sent(field):
        for side in (-1, 1):
            @pl.when(aa_there(side))
            def _():
                for piece in range(3):
                    along_time(field, side, piece).wait_send()

            pl.when(ba_there(side))(along_rows(field, 1, side).wait_send)
            for frame, behind in ((0, -1), (2, 1)):
                pl.when(jnp.logical_and(aa_there(behind), ba_there(side)))(
                    along_rows(field, frame, side).wait_send
                )

    def blank(field):
        line = jnp.zeros((width, chans), BF16)
        for frame, behind in ((0, -1), (2, 1)):
            @pl.when(jnp.logical_not(aa_there(behind)))
            def _():
                for row in range(rows + 2):
                    field[frame, row] = line

            @pl.when(aa_there(behind))
            def _():
                for side, row in ((-1, 0), (1, rows + 1)):
                    @pl.when(jnp.logical_not(ba_there(side)))
                    def _():
                        field[frame, row] = line
        for side, row in ((-1, 0), (1, rows + 1)):
            @pl.when(jnp.logical_not(ba_there(side)))
            def _():
                field[1, row] = line

    blank(field_one)
    blank(field_two)
    pl.semaphore_wait(barrier, n_aa - 1 + n_ba - 1)
    loads[0].wait()
    send_field(field_one)

    def merge_weights():
        embed = embed_weight[...].astype(F32)
        centred = jnp.concatenate(
            [
                embed - embed.mean(-1, keepdims=True),
                jnp.broadcast_to(
                    embed_bias[...] - embed_bias[...].mean(-1, keepdims=True),
                    (8, embed.shape[1]),
                ),
            ],
            axis=0,
        )
        gram[...] = lax.dot_general(
            centred, centred, (((1,), (1,)), ((), ())),
            precision=lax.Precision.HIGHEST, preferred_element_type=F32,
        ) * (1.0 / embed.shape[1])
        high, low = two_parts(gram[:lat, :lat])
        gram_split[:lat] = high
        gram_split[lat:] = low
        gained_high, gained_low = two_parts(centred * norm_gain[...])
        for which in range(3):
            loads[2 + which].wait()
            product = dot(gained_high, w_joined[which]) + dot(gained_low, w_joined[which])
            if which == 0:
                product = product * (HEAD_DIM**-0.5 * math.log2(math.e))
            blanks = jnp.zeros((product.shape[0], SLOT - HEAD_DIM), F32)
            for head in range(heads):
                piece = jnp.concatenate(
                    [product[:, head * HEAD_DIM : (head + 1) * HEAD_DIM], blanks], axis=1
                )
                slot = slice(head * SLOT, (head + 1) * SLOT)
                high, low = two_parts(piece[:lat])
                split[which, :lat, slot] = high
                split[which, lat:, slot] = low
                offsets[which, :, slot] = piece[lat:]

    def convolve(field, bias, filler):
        def tap(shift_t, shift_r, first):
            window = field[shift_t, pl.ds(shift_r, rows)].reshape(rows * width, chans)
            for shift_w in range(3):
                part = dot(window, taps[(shift_t * 3 + shift_r) * 3 + shift_w])
                if first:
                    acc[shift_w] = part
                else:
                    acc[shift_w] += part

        tap(1, 1, True)
        take_rows(field, 1)
        tap(1, 0, False)
        tap(1, 2, False)
        take_time(field, (0, 1))
        relay_rows(field)
        filler()
        take_time(field, (2,))
        tap(0, 1, False)
        tap(2, 1, False)
        take_rows(field, 0)
        take_rows(field, 2)

        @pl.loop(0, 2)
        def _(index):
            tap(0, 2 * index, False)
            tap(2, 2 * index, False)

        total = acc[1] + bias
        place = lax.broadcasted_iota(jnp.int32, total.shape, 0) % width
        total += jnp.where(place == 0, 0.0, pltpu.roll(acc[0], 1, 0))
        total += jnp.where(place == width - 1, 0.0, pltpu.roll(acc[2], rows * width - 1, 0))
        return total

    loads[1].wait()
    first = gelu(convolve(field_one, bias_one[...], merge_weights)).astype(BF16)
    field_two[1, 1 : rows + 1] = first.reshape(rows, width, chans)
    send_field(field_two)
    again = load(conv_two, taps, 5)
    again.start()
    again.wait()
    total = convolve(field_two, bias_two[...], lambda: None)
    own = field_two[1, 1 : rows + 1].reshape(rows * width, chans).astype(F32)
    second = (own + gelu(total)).astype(BF16)

    line = width // 2
    for block in range(rows // 2):
        upper = second[(2 * block) * width : (2 * block + 1) * width]
        lower = second[(2 * block + 1) * width : (2 * block + 2) * width]
        for col in range(2):
            pair[col] = dot(upper, patch_weight[0, col]) + dot(lower, patch_weight[1, col])
        patches = (
            pair[0, pl.ds(0, line, stride=2), :] + pair[1, pl.ds(1, line, stride=2), :]
            + patch_bias[...]
        ).astype(BF16)
        gathered[ba, pl.ds(pl.multiple_of(aa * tokens + block * line, line), line), :] = patches

    def along_aa(step):
        block = gathered.at[ba, pl.ds(pl.multiple_of(aa * tokens, tokens), tokens)]
        return pltpu.make_async_remote_copy(
            src_ref=block, dst_ref=block, send_sem=aa_send.at[step], recv_sem=aa_recv.at[step],
            device_id=((aa + step) % n_aa, ba), device_id_type=MESH,
        )

    def along_ba(step):
        return pltpu.make_async_remote_copy(
            src_ref=gathered.at[ba], dst_ref=gathered.at[ba],
            send_sem=ba_send.at[step], recv_sem=ba_recv.at[step],
            device_id=(aa, (ba + 2 * step) % n_ba), device_id_type=MESH,
        )

    def to_partner(step):
        block = gathered.at[(ba + n_ba - 2 * step) % n_ba]
        return pltpu.make_async_remote_copy(
            src_ref=block, dst_ref=block, send_sem=core_send.at[step], recv_sem=core_recv.at[step],
            device_id=(aa, partner), device_id_type=MESH,
        )

    slope = 2.0 * gram[lat : lat + 1, :lat]
    floor = gram[lat : lat + 1, lat : lat + 1]
    column = lax.broadcasted_iota(jnp.int32, (n_aa * tokens, SLOT), 1)

    def spread_of(latents, twice):
        bent = dot(twice, gram_split[...]) + slope
        power = (bent * latents.astype(F32)).sum(-1, keepdims=True) + floor
        return lax.rsqrt(jnp.maximum(power, 0.0) + 1e-05)

    def project(twice, scale, which):
        return ((dot(twice, split[which]) + offsets[which, :1]) * scale).astype(BF16)

    def take_block(block):
        latents = gathered[block]
        twice = jnp.concatenate([latents, latents], axis=1)
        scale = spread_of(latents, twice)
        projected_keys = project(twice, scale, 1)
        projected_values = project(twice, scale, 2)
        length = n_aa * tokens
        where = pl.ds(pl.multiple_of(block * length, length), length)
        for head in range(heads):
            keys[head, where] = projected_keys[:, head * SLOT : (head + 1) * SLOT]
            values[head, where] = jnp.where(
                column == HEAD_DIM,
                jnp.ones((), BF16),
                projected_values[:, head * SLOT : (head + 1) * SLOT],
            )
        mine = gathered[block, pl.ds(pl.multiple_of(aa * tokens, tokens), tokens)]
        twice = jnp.concatenate([mine, mine], axis=1)
        asked = project(twice, spread_of(mine, twice), 0)
        there = pl.ds(pl.multiple_of(block * tokens, tokens), tokens)
        for head in range(heads):
            queries[head, there] = asked[:, head * SLOT : (head + 1) * SLOT]

    for step in range(1, n_aa):
        along_aa(step).start()
    sent(field_one)
    sent(field_two)
    for step in range(1, n_aa):
        along_aa(step).wait_recv()
    for step in range(1, half):
        along_ba(step).start()
    to_partner(0).start()
    take_block(ba)
    to_partner(0).wait_recv()
    take_block(partner)

    @pl.loop(1, half)
    def _(step):
        along_ba(step).wait_recv()
        to_partner(step).start()
        take_block((ba + n_ba - 2 * step) % n_ba)

    @pl.loop(1, half)
    def _(step):
        to_partner(step).wait_recv()
        take_block((partner + n_ba - 2 * step) % n_ba)

    for step in range(1, n_aa):
        along_aa(step).wait_send()
    for step in range(1, half):
        along_ba(step).wait_send()
    for step in range(half):
        to_partner(step).wait_send()

    def share(dest):
        offset = (dest + n_ba - ba) % n_ba
        return pltpu.make_async_remote_copy(
            src_ref=shares.at[dest], dst_ref=arrived.at[ba],
            send_sem=share_send.at[offset], recv_sem=share_recv.at[offset],
            device_id=(aa, dest), device_id_type=MESH,
        )

    per_span = span // tokens
    spans = n_ba // per_span
    total = keys.shape[1]
    big = math.gcd(total, 4096)

    @pl.loop(0, spans)
    def _(step):
        at = (ba // per_span + 1 + step) % spans
        where = pl.ds(pl.multiple_of(at * span, span), span)

        def one_head(head, velocity):
            asked = queries[head, where]

            def one_big(index, state):
                best, accum = state
                for piece in range(big // chunk):
                    held = pl.ds(pl.multiple_of(index * big + piece * chunk, chunk), chunk)
                    scores = lax.dot_general(
                        asked, keys[head, held], (((1,), (1,)), ((), ())),
                        preferred_element_type=F32,
                    )
                    peak = jnp.maximum(best, scores.max(-1, keepdims=True))
                    probs = jnp.exp2(scores - peak).astype(BF16)
                    accum = accum * jnp.exp2(best - peak) + dot(probs, values[head, held])
                    best = peak
                return best, accum

            state = (jnp.full((span, 1), -jnp.inf, F32), jnp.zeros((span, SLOT), F32))
            if total == big:
                _, accum = one_big(0, state)
            else:
                _, accum = lax.fori_loop(0, total // big, one_big, state)
            attended = (accum[:, :HEAD_DIM] / accum[:, HEAD_DIM : HEAD_DIM + 1]).astype(BF16)
            rows = pl.ds(pl.multiple_of(head * HEAD_DIM, HEAD_DIM), HEAD_DIM)
            return velocity + dot(attended, w_velocity[rows])

        velocity = lax.fori_loop(0, heads, one_head, jnp.zeros((span, w_velocity.shape[1]), F32), unroll=2)
        for part in range(per_span):
            dest = at * per_span + part
            shares[dest] = velocity[part * tokens : (part + 1) * tokens].astype(BF16)

            @pl.when(dest != ba)
            def _():
                share(dest).start()

    summed = shares[ba].astype(F32)
    for offset in range(1, n_ba):
        share((ba + offset) % n_ba).wait_recv()
        summed += arrived[(ba + n_ba - offset) % n_ba].astype(F32)
    out[...] = summed
    for offset in range(1, n_ba):
        share((ba + offset) % n_ba).wait_send()


def on_device(
    n_aa, n_ba,
    feats, conv_one, bias_one, conv_two, bias_two, patch_weight, patch_bias,
    embed_weight, embed_bias, norm_gain, w_query, w_key, w_value, w_velocity,
):
    _, rows, width, chans = feats.shape
    lat = patch_bias.shape[0]
    features, qwidth = w_query.shape
    heads = qwidth // HEAD_DIM
    tokens = rows * width // 4
    total = n_ba * n_aa * tokens
    span = max(tokens, min(512, n_ba * tokens))
    chunk = math.gcd(total, 2048)
    vmem = pl.BlockSpec(memory_space=pltpu.VMEM)
    anywhere = pl.BlockSpec(memory_space=pl.ANY)
    dma = pltpu.SemaphoreType.DMA
    return pl.pallas_call(
        functools.partial(whole_kernel, n_aa, n_ba, span, chunk),
        out_shape=jax.ShapeDtypeStruct((tokens, lat), F32),
        in_specs=[anywhere, anywhere, vmem, anywhere] + [vmem] * 6 + [anywhere] * 3 + [vmem],
        out_specs=vmem,
        scratch_shapes=[
            pltpu.VMEM((3, rows + 2, width, chans), BF16),
            pltpu.VMEM((3, rows + 2, width, chans), BF16),
            pltpu.VMEM((27, chans, chans), BF16),
            pltpu.VMEM((3, features, qwidth), BF16),
            pltpu.VMEM((3, rows * width, chans), F32),
            pltpu.VMEM((2, width, lat), F32),
            pltpu.VMEM((n_ba, n_aa * tokens, lat), BF16),
            pltpu.VMEM((3, 2 * lat, heads * SLOT), BF16),
            pltpu.VMEM((3, 8, heads * SLOT), F32),
            pltpu.VMEM((2 * lat, lat), BF16),
            pltpu.VMEM((lat + 8, lat + 8), F32),
            pltpu.VMEM((heads, n_ba * tokens, SLOT), BF16),
            pltpu.VMEM((heads, total, SLOT), BF16),
            pltpu.VMEM((heads, total, SLOT), BF16),
            pltpu.VMEM((n_ba, tokens, lat), BF16),
            pltpu.VMEM((n_ba, tokens, lat), BF16),
            dma((6,)),
            dma((2, 2, 3)), dma((2, 2, 3)), dma((2, 3, 2)), dma((2, 3, 2)),
            dma((n_aa,)), dma((n_aa,)),
            dma((n_ba // 2,)), dma((n_ba // 2,)),
            dma((n_ba // 2,)), dma((n_ba // 2,)),
            dma((n_ba,)), dma((n_ba,)),
        ],
        compiler_params=pltpu.CompilerParams(
            collective_id=0, has_side_effects=True, vmem_limit_bytes=VMEM_BYTES
        ),
        name="whole",
    )(
        feats, conv_one.reshape(27, chans, chans), bias_one[None],
        conv_two.reshape(27, chans, chans), bias_two[None],
        patch_weight, patch_bias[None], embed_weight, embed_bias[None], norm_gain[None],
        w_query, w_key, w_value, w_velocity,
    )


def solution(mesh):
    return jax.shard_map(
        functools.partial(on_device, mesh.shape["aa"], mesh.shape["ba"]),
        mesh=mesh,
        in_specs=(
            P("aa", "ba", None, None), P(), P(), P(), P(), P(), P(), P(), P(), P(),
            P(None, "ba"), P(None, "ba"), P(None, "ba"), P("ba", None),
        ),
        out_specs=P(("aa", "ba"), None),
        check_vma=False,
    )
```
